32 devices in a mesh: row: 4 (over y, x), col: 4 (over z), depth: 2 (over core).
Axes of the slice: x: 2, y: 2, z: 4, core: 2. Of those that a mesh axis runs over, the one named last changes fastest.
Arguments:
- matrix_panel: bfloat16 [12288, 65536], P('row', 'col'), may hold values from -0.1484375 to 0.1484375
- start_block: bfloat16 [12288, 64], P('row', 'depth'), may hold values from -6 to 6
- stored_basis: float32 [12288, 1024], P('row'), may hold values from -2.2 to 2.2
Outputs:
- new_block: float32 [12288, 64], P('row', 'depth')
- coefficients: float32 [1024, 64], P(None, 'depth')
- triangle: float32 [64, 64], replicated
The draws below stay inside these ranges and needn't reach their ends.
All inputs are finite; a program needn't handle non-finite values.
Results may differ from the reference program's by a relative error of at most 0.0023.
Values may be sent and summed in bfloat16 or wider, within the bound.
A program may use at most 256 MiB of HBM per device.

```python
import jax
import jax.numpy as jnp
from jax import lax

N = 65536
K = 1024
B = 64
M = 12288


def basis_values(key):
    key_signs, key_codes, key_noise = jax.random.split(jax.random.fold_in(key, 23), 3)
    row_ids = jnp.arange(M, dtype=jnp.int32)[:, None]
    codes = jax.random.permutation(key_codes, K).astype(jnp.int32)[None, :]
    shared = jnp.bitwise_and(row_ids, codes)
    parity = jnp.zeros((M, K), jnp.int32)
    for shift_count in range(24):
        parity = parity + jnp.bitwise_and(jnp.right_shift(shared, shift_count), 1)
    parity = jnp.bitwise_and(parity, 1)
    row_signs = jax.random.randint(key_signs, (M, 1), 0, 2).astype(jnp.int32) * 2 - 1
    walsh = (row_signs * (1 - 2 * parity)).astype(jnp.float32)
    noise = 0.2 * jnp.clip(jax.random.normal(key_noise, (M, K)), -6.0, 6.0)
    return (walsh + noise).astype(jnp.float32)


def draw_matrix_panel(key, part):
    key_noise, key_rows, key_cols, key_mix = jax.random.split(jax.random.fold_in(key, 11), 4)
    basis = basis_values(key)
    position = jnp.arange(M, dtype=jnp.float32)[:, None] / (M - 1)
    row_factor = jnp.exp(0.6 * jax.random.uniform(key_rows, (M, 1), minval=-1.0, maxval=1.0)) * jnp.sqrt(1.0 + position)
    col_factor = jnp.exp(jnp.log(10.0) * (jax.random.uniform(key_cols, (1, N)) - 0.5))
    mix_values = jnp.clip(jax.random.normal(key_mix, (K, N)), -6.0, 6.0)
    coupling = 2.2 * (float(N + M) / float(K)) ** 0.25 / float(N * M) ** 0.5
    mix_values = (mix_values * col_factor * coupling).astype(jnp.float32)
    noise_scale = 1.0 / (2.0 * float(N * M) ** 0.25)

    def block_rows(block_index):
        first_row = (block_index * K).astype(jnp.int32)
        block_key = jax.random.fold_in(key_noise, block_index)
        noise = jnp.clip(jax.random.normal(block_key, (K, N)), -6.0, 6.0)
        rows_scale = lax.dynamic_slice_in_dim(row_factor, first_row, K, 0)
        rows_basis = lax.dynamic_slice_in_dim(basis, first_row, K, 0)
        along = jnp.dot(rows_basis, mix_values, precision=lax.Precision.HIGHEST, preferred_element_type=jnp.float32)
        values = noise * rows_scale * col_factor * noise_scale + along
        values = jnp.clip(values, -0.1484375, 0.1484375)
        return values.astype(jnp.bfloat16)
    blocks = lax.map(block_rows, jnp.arange(M // K, dtype=jnp.int32))
    return blocks.reshape(M, N)


def draw_stored_basis(key, part):
    return basis_values(key)


def shard_levels(own_key, shape, cuts, low, high):
    def one(dim, shards_of):
        steps = jax.random.uniform(jax.random.fold_in(jax.random.fold_in(own_key, 6), dim), (shards_of,), jnp.float32, low / len(cuts), high / len(cuts))
        return jnp.repeat(jnp.exp(steps), shape[dim] // shards_of).reshape((-1,) + (1,) * (len(shape) - dim - 1))

    gain = one(*cuts[0])
    for cut in cuts[1:]:
        gain = gain * one(*cut)
    return gain


def centred(rng, shape, scale, most, cuts=(), kind=jnp.bfloat16):
    result = jax.random.normal(rng, shape, jnp.float32) * scale
    if len(cuts) > 0:
        result = shard_levels(rng, shape, cuts, -0.22, 0.18) * result
    return jnp.clip(result, min=-most, max=most).astype(kind)


def setup_inputs(seed: int = 0) -> dict:
    key_list = jax.random.split(jax.random.key(seed), 4)
    matrix_panel = draw_matrix_panel(jax.random.fold_in(key_list[3], 71), 0)
    start_block = centred(key_list[1], (M, B), 1.0, 6.0, ((0, 4), (1, 2)))
    stored_basis = draw_stored_basis(jax.random.fold_in(key_list[3], 71), 0)
    return dict(matrix_panel=matrix_panel, start_block=start_block, stored_basis=stored_basis)


HIGHEST = lax.Precision.HIGHEST

def factor_gram(gram_matrix):
    lower_factor = jnp.linalg.cholesky(gram_matrix)
    identity = jnp.eye(gram_matrix.shape[0], dtype=jnp.float32)
    inverse = jax.scipy.linalg.solve_triangular(lower_factor, identity, lower=True)
    return (lower_factor, inverse)

def orthonormal_pass(stored_basis, block_cols):
    projection = jnp.dot(stored_basis.T.astype(jnp.float32), block_cols.astype(jnp.float32), precision=HIGHEST, preferred_element_type=jnp.float32) / M
    remainder = block_cols - jnp.dot(stored_basis.astype(jnp.float32), projection.astype(jnp.float32), precision=HIGHEST, preferred_element_type=jnp.float32)
    gram_matrix = jnp.dot(remainder.T.astype(jnp.float32), remainder.astype(jnp.float32), precision=HIGHEST, preferred_element_type=jnp.float32) / M
    lower_factor, inverse = factor_gram(gram_matrix)
    normed = jnp.dot(remainder.astype(jnp.float32), inverse.T.astype(jnp.float32), precision=HIGHEST, preferred_element_type=jnp.float32)
    return (projection, lower_factor, normed)

def reference(matrix_panel, start_block, stored_basis):
    mixed_cols = jnp.dot(matrix_panel.T.astype(jnp.float32), start_block.astype(jnp.float32), preferred_element_type=jnp.float32).astype(jnp.bfloat16)
    image_block = jnp.dot(matrix_panel.astype(jnp.float32), mixed_cols.astype(jnp.float32), preferred_element_type=jnp.float32)
    proj_first, lower_first, normed_first = orthonormal_pass(stored_basis, image_block)
    proj_second, lower_second, new_block = orthonormal_pass(stored_basis, normed_first)
    coefficients = proj_first + jnp.dot(proj_second.astype(jnp.float32), lower_first.T.astype(jnp.float32), precision=HIGHEST, preferred_element_type=jnp.float32)
    triangle = jnp.dot(lower_second.T.astype(jnp.float32), lower_first.T.astype(jnp.float32), precision=HIGHEST, preferred_element_type=jnp.float32)
    return (new_block, coefficients, triangle)
```

```python
import functools

import jax
import jax.numpy as jnp
from jax import lax
from jax.experimental import pallas as pl
from jax.experimental.pallas import tpu as pltpu
from jax.sharding import PartitionSpec as P

HIGHEST = lax.Precision.HIGHEST
MESH = pl.DeviceIdType.MESH
F32 = jnp.float32
LANES = 128
LOOK = 4


def mm(a, b, precision=HIGHEST):
    return lax.dot_general(
        a, b, (((1,), (0,)), ((), ())), precision=precision, preferred_element_type=F32
    )


def mm_nt(a, b, precision=HIGHEST):
    return lax.dot_general(
        a, b, (((1,), (1,)), ((), ())), precision=precision, preferred_element_type=F32
    )


def factor(gram_twice):
    size = gram_twice.shape[0]
    rows = lax.broadcasted_iota(jnp.int32, (size, 2 * size), 0)
    lanes = lax.broadcasted_iota(jnp.int32, (size, 2 * size), 1)
    work = jnp.where(lanes < size, gram_twice, jnp.where(lanes - size == rows, 1.0, 0.0))

    def step(k, carry):
        work, pivots = carry
        at_lane = lanes == k
        at_row = rows == k
        column = jnp.sum(jnp.where(at_lane, work, 0.0), axis=1, keepdims=True)
        row = jnp.sum(jnp.where(at_row, work, 0.0), axis=0, keepdims=True)
        pivot_row = jnp.sum(jnp.where(at_lane & at_row, work, 0.0), axis=0, keepdims=True)
        pivot = jnp.sum(pivot_row, axis=1, keepdims=True)
        scale = column / pivot
        work = work - jnp.where(rows > k, scale * row, 0.0)
        pivots = jnp.where(at_row, pivot, pivots)
        return (work, pivots)

    work, pivots = lax.fori_loop(0, size, step, (work, jnp.ones_like(work)))
    work = work / jnp.sqrt(pivots)
    upper = jnp.where(rows <= lanes, work, 0.0)[:, :size]
    return (upper, work[:, size:])


def krylov_kernel(
    dims,
    panel_ref,
    start_ref,
    basis_ref,
    new_ref,
    coef_ref,
    tri_ref,
    held,
    start_all,
    part,
    gathered,
    image,
    sib_buf,
    col_buf,
    basis,
    proj_part,
    proj_in,
    proj_col,
    proj_all,
    gram_in,
    gram_col,
    out_part,
    out_buf,
    *rest,
):
    n_row, n_col, total_rows = dims
    stages = n_row.bit_length() - 1
    recvs = rest[:stages]
    (panel_sem, mix_send, mix_recv, misc_sem, sib_sem, col_send, col_recv,
     p_send, p_recv, z_send, z_recv, a_send, a_recv, g_send, g_recv, h_send, h_recv,
     o_send, o_recv) = rest[stages:]
    chunks, rows_here, width = held.shape
    cols = start_all.shape[0] * start_all.shape[1]
    pieces = image.shape[0]
    piece = image.shape[2]
    n_plane = n_row * 2
    row = lax.axis_index("row")
    col = lax.axis_index("col")
    core = lax.axis_index("depth")
    inv_total = 1.0 / total_rows

    def bit_of(value, bit):
        return (value // (1 << bit)) % 2

    def pick(first, second):
        return first * (1 - core) + second * core

    partners = []
    order = 0
    for s in range(stages):
        flips = [row + (1 - 2 * bit_of(row, b)) * (1 << b) for b in (s, stages - 1 - s)]
        partners.append(pick(flips[0], flips[1]))
        bits = pick(bit_of(row, s), bit_of(row, stages - 1 - s))
        order = order * 2 + bits
    plane_me = row * 2 + core
    col_group_me = core * n_col + col

    def plane_device(j):
        target = (plane_me + j) % n_plane
        return target, {"row": target // 2, "depth": target % 2}

    def col_device(j):
        target = (col + j) % n_col
        return target, {"col": target}

    def group_device(j):
        target = (col_group_me + j) % pieces
        return target, {"col": target % n_col, "depth": target // n_col}

    def panel_copy(t):
        first = pl.multiple_of((core * chunks + t) * width, width)
        return pltpu.make_async_copy(
            panel_ref.at[:, pl.ds(first, width)], held.at[t], panel_sem.at[t]
        )

    for t in range(min(LOOK, chunks)):
        panel_copy(t).start()

    basis_first = pl.multiple_of(col_group_me * piece, 8)
    basis_copy = pltpu.make_async_copy(
        basis_ref.at[pl.ds(basis_first, piece), :], basis, misc_sem.at[0]
    )
    own_start = pltpu.make_async_copy(start_ref, start_all.at[core], misc_sem.at[1])
    own_start.start()

    barrier = pltpu.get_barrier_semaphore()
    greeted = 0
    for j in range(1, n_plane):
        pl.semaphore_signal(barrier, inc=1, device_id=plane_device(j)[1], device_id_type=MESH)
        greeted += 1
    for j in range(1, pieces):
        pl.semaphore_signal(barrier, inc=1, device_id=group_device(j)[1], device_id_type=MESH)
        greeted += 1
    pl.semaphore_wait(barrier, greeted)

    def remote(src, dst, send_sem, recv_sem, device):
        return pltpu.make_async_remote_copy(
            src_ref=src,
            dst_ref=dst,
            send_sem=send_sem,
            recv_sem=recv_sem,
            device_id=device,
            device_id_type=MESH,
        )

    sibling = {"depth": 1 - core}
    start_copy = remote(start_ref, start_all.at[core], sib_sem.at[0], sib_sem.at[1], sibling)
    start_copy.start()
    image[...] = jnp.zeros_like(image)
    own_start.wait()
    start_copy.wait()

    def span(s):
        length = n_row >> s
        return (order // length) * length, length

    def reduce_copy(s, t):
        first, length = span(s)
        half = length // 2
        mine = span(s + 1)[0]
        other = first + (first + half - mine)
        return remote(
            part.at[t, pl.ds(other, half)],
            recvs[s].at[t],
            mix_send.at[s, t],
            mix_recv.at[s, t],
            {"row": partners[s]},
        )

    def gather_copy(s, t):
        level = stages - 1 - s
        first, length = span(level + 1)
        region = gathered.at[t, pl.ds(first, length)]
        return remote(
            region, region, mix_send.at[stages + s, t], mix_recv.at[stages + s, t],
            {"row": partners[level]},
        )

    block = rows_here // 4
    per_block = block // piece

    def body(i, carry):
        for s in reversed(range(stages)):
            t = i - (stages + 1 + s)

            if s < stages - 1:
                @pl.when((t >= 0) & (t < chunks))
                def _():
                    gather_copy(s, t).wait_recv()
                    gather_copy(s + 1, t).start()

        for s in reversed(range(stages)):
            t = i - (s + 1)

            @pl.when((t >= 0) & (t < chunks))
            def _():
                reduce_copy(s, t).wait_recv()
                first, length = span(s + 1)
                summed = part[t, pl.ds(first, length)] + recvs[s][t]
                if s < stages - 1:
                    part[t, pl.ds(first, length)] = summed
                    reduce_copy(s + 1, t).start()
                else:
                    gathered[t, pl.ds(first, length)] = summed.astype(jnp.bfloat16)
                    gather_copy(0, t).start()

        @pl.when(i < chunks)
        def _():
            @pl.when(i + LOOK < chunks)
            def _():
                panel_copy(i + LOOK).start()

            panel_copy(i).wait()
            lhs = start_all[...].reshape(cols, rows_here)
            mixed = mm(lhs, held[i], None)
            for p in range(n_row):
                part[i, p] = mixed[:, p * LANES : (p + 1) * LANES]
            reduce_copy(0, i).start()

        t = i - 2 * stages

        @pl.when(t >= 0)
        def _():
            gather_copy(stages - 1, t).wait_recv()
            lhs = jnp.concatenate([gathered[t, p] for p in range(n_row)], axis=1)
            for h in range(4):
                got = mm_nt(lhs, held[t, h * block : (h + 1) * block, :], None)
                for q in range(per_block):
                    image[h * per_block + q] += got[:, q * piece : (q + 1) * piece]

        return carry

    lax.fori_loop(0, chunks + 2 * stages, body, 0)
    basis_copy.start()

    half_copy = remote(
        image.at[pl.ds((1 - core) * n_col, n_col)], sib_buf, sib_sem.at[2], sib_sem.at[3], sibling
    )
    half_copy.start()
    half_copy.wait()
    sib_buf[...] = sib_buf[...] + image[pl.ds(core * n_col, n_col)]
    copies = []
    for j in range(1, n_col):
        target, device = col_device(j)
        copies.append(
            remote(sib_buf.at[target], col_buf.at[col], col_send.at[j], col_recv.at[j], device)
        )
        copies[-1].start()
    col_buf[col] = sib_buf[col]

    def drain(t, carry):
        for s in range(stages):
            reduce_copy(s, t).wait_send()
            gather_copy(s, t).wait_send()
        return carry

    lax.fori_loop(0, chunks, drain, 0)
    basis_copy.wait()
    for copy in copies:
        copy.wait()

    image_t = col_buf[0]
    for c in range(1, n_col):
        image_t = image_t + col_buf[c]

    k_total = basis.shape[1]
    piece_rows, piece_lanes = proj_part.shape[1:]
    lane_blocks = k_total // piece_lanes

    def start_plane(slot, src_of, dst, send, recv):
        made = []
        for j in range(1, n_plane):
            target, device = plane_device(j)
            made.append(remote(src_of(target), dst, send.at[slot, j], recv.at[slot, j], device))
            made[-1].start()
        return made

    def start_cols(slot, src, dst, send, recv):
        made = []
        for j in range(1, n_col):
            target, device = col_device(j)
            made.append(remote(src, dst, send.at[slot, j], recv.at[slot, j], device))
            made[-1].start()
        return made

    def finish(made):
        for copy in made:
            copy.wait()

    def ordered_sum(ref, slot, count):
        total = ref[slot, 0]
        for c in range(1, count):
            total = total + ref[slot, c]
        return total

    def project_start(slot, value):
        for p in range(n_plane):
            lane = (p % lane_blocks) * piece_lanes
            top = (p // lane_blocks) * piece_rows
            proj_part[p] = value[top : top + piece_rows, lane : lane + piece_lanes]
        copies = start_plane(
            slot, lambda target: proj_part.at[target], proj_in.at[slot, plane_me], p_send, p_recv
        )
        proj_in[slot, plane_me] = proj_part[plane_me]
        return copies

    def project_mid(slot, copies):
        finish(copies)
        proj_col[slot, col] = ordered_sum(proj_in, slot, n_plane)
        mine = proj_col.at[slot, col]
        return start_cols(slot, mine, mine, z_send, z_recv)

    def project_end(slot, copies):
        finish(copies)
        proj_all[slot, plane_me] = ordered_sum(proj_col, slot, n_col) * inv_total
        mine = proj_all.at[slot, plane_me]
        return start_plane(slot, lambda target: mine, mine, a_send, a_recv)

    def project_value(slot):
        bands = []
        for top in range(n_plane // lane_blocks):
            bands.append(
                jnp.concatenate(
                    [proj_all[slot, top * lane_blocks + p] for p in range(lane_blocks)], axis=1
                )
            )
        return jnp.concatenate(bands, axis=0) if len(bands) > 1 else bands[0]

    def gram_start(slot, value):
        gram_in[slot, plane_me] = mm_nt(value, jnp.concatenate([value, value], axis=0))
        mine = gram_in.at[slot, plane_me]
        return start_plane(slot, lambda target: mine, mine, g_send, g_recv)

    def gram_mid(slot, copies):
        finish(copies)
        gram_col[slot, col] = ordered_sum(gram_in, slot, n_plane)
        mine = gram_col.at[slot, col]
        return start_cols(slot, mine, mine, h_send, h_recv)

    def gram_end(slot, copies):
        finish(copies)
        return ordered_sum(gram_col, slot, n_col) * inv_total

    copies = project_start(0, mm(image_t, basis[...]))
    copies = project_mid(0, copies)
    finish(project_end(0, copies))
    proj_first = project_value(0)
    remainder = image_t - mm_nt(proj_first, basis[...])

    gram_copies = gram_start(0, remainder)
    copies = project_start(1, mm(remainder, basis[...]))
    gram_copies = gram_mid(0, gram_copies)
    copies = project_mid(1, copies)
    gram_first = gram_end(0, gram_copies)
    copies = project_end(1, copies)
    upper_first, inverse_first = factor(gram_first)
    finish(copies)
    proj_second = project_value(1)
    coef = proj_first + proj_second
    half = coef_ref.shape[0]
    proj_second_rem = remainder - mm_nt(proj_second, basis[...])
    second = mm(inverse_first, proj_second_rem)

    gram_copies = gram_start(1, second)

    @pl.when(core == 0)
    def _():
        coef_ref[...] = coef[:half]

    @pl.when(core == 1)
    def _():
        coef_ref[...] = coef[half:]

    gram_copies = gram_mid(1, gram_copies)
    gram_second = gram_end(1, gram_copies)
    upper_second, inverse_second = factor(gram_second)
    new_t = mm(inverse_second, second)
    out_part[0] = new_t[:half]
    out_part[1] = new_t[half:]
    copies = []
    for j in range(1, pieces):
        target, device = group_device(j)
        copies.append(
            remote(
                out_part.at[target // n_col], out_buf.at[col_group_me],
                o_send.at[j], o_recv.at[j], device,
            )
        )
        copies[-1].start()
    out_buf[col_group_me] = out_part[core]
    tri_ref[...] = mm(upper_second, upper_first)
    finish(copies)
    for q in range(pieces):
        new_ref[:, q * piece : (q + 1) * piece] = out_buf[q]


def per_device(matrix_panel, start_block, stored_basis):
    n_row = lax.axis_size("row")
    n_col = lax.axis_size("col")
    n_core = lax.axis_size("depth")
    rows_here, cols_here = matrix_panel.shape
    half = start_block.shape[1]
    cols = half * n_core
    k_total = stored_basis.shape[1]
    stages = n_row.bit_length() - 1
    width = LANES * n_row
    chunks = cols_here // n_core // width
    pieces = n_col * n_core
    piece = rows_here // pieces
    n_plane = n_row * n_core
    piece_lanes = max(LANES, k_total // n_plane)
    piece_rows = cols * k_total // (n_plane * piece_lanes)
    dma = pltpu.SemaphoreType.DMA
    scratch = [
        pltpu.VMEM((chunks, rows_here, width), jnp.bfloat16),
        pltpu.VMEM((n_core, half, rows_here), jnp.bfloat16),
        pltpu.VMEM((chunks, n_row, cols, LANES), F32),
        pltpu.VMEM((chunks, n_row, cols, LANES), jnp.bfloat16),
        pltpu.VMEM((pieces, cols, piece), F32),
        pltpu.VMEM((n_col, cols, piece), F32),
        pltpu.VMEM((n_col, cols, piece), F32),
        pltpu.VMEM((piece, k_total), F32),
        pltpu.VMEM((n_plane, piece_rows, piece_lanes), F32),
        pltpu.VMEM((2, n_plane, piece_rows, piece_lanes), F32),
        pltpu.VMEM((2, n_col, piece_rows, piece_lanes), F32),
        pltpu.VMEM((2, n_plane, piece_rows, piece_lanes), F32),
        pltpu.VMEM((2, n_plane, cols, 2 * cols), F32),
        pltpu.VMEM((2, n_col, cols, 2 * cols), F32),
        pltpu.VMEM((n_core, half, piece), F32),
        pltpu.VMEM((pieces, half, piece), F32),
    ]
    scratch += [
        pltpu.VMEM((chunks, n_row >> (s + 1), cols, LANES), F32) for s in range(stages)
    ]
    scratch += [
        dma((chunks,)),
        dma((2 * stages, chunks)),
        dma((2 * stages, chunks)),
        dma((2,)),
        dma((4,)),
        dma((n_col,)),
        dma((n_col,)),
        dma((2, n_plane)),
        dma((2, n_plane)),
        dma((2, n_col)),
        dma((2, n_col)),
        dma((2, n_plane)),
        dma((2, n_plane)),
        dma((2, n_plane)),
        dma((2, n_plane)),
        dma((2, n_col)),
        dma((2, n_col)),
        dma((pieces,)),
        dma((pieces,)),
    ]
    whole = pl.BlockSpec(memory_space=pltpu.VMEM)
    hbm = pl.BlockSpec(memory_space=pl.ANY)
    new_t, coef_t, triangle = pl.pallas_call(
        functools.partial(krylov_kernel, (n_row, n_col, rows_here * n_row)),
        out_shape=(
            jax.ShapeDtypeStruct((half, rows_here), F32),
            jax.ShapeDtypeStruct((half, k_total), F32),
            jax.ShapeDtypeStruct((cols, cols), F32),
        ),
        in_specs=[hbm, whole, hbm],
        out_specs=(whole, whole, whole),
        scratch_shapes=scratch,
        compiler_params=pltpu.CompilerParams(
            collective_id=0, has_side_effects=True, vmem_limit_bytes=63 << 20
        ),
    )(matrix_panel, start_block.T, stored_basis)
    return (new_t.T, coef_t.T, triangle)


def solution(mesh):
    placed = (P("row", "col"), P("row", "depth"), P("row", None))
    return jax.shard_map(
        per_device,
        mesh=mesh,
        in_specs=placed,
        out_specs=(P("row", "depth"), P(None, "depth"), P()),
        check_vma=False,
    )
```

```python
import functools

import jax
import jax.numpy as jnp
from jax import lax
from jax.experimental import pallas as pl
from jax.experimental.pallas import tpu as pltpu
from jax.sharding import PartitionSpec as P

HIGHEST = lax.Precision.HIGHEST
MESH = pl.DeviceIdType.MESH
F32 = jnp.float32
LANES = 128
LOOK = 4
LAG = 3


def mm(a, b, precision=HIGHEST):
    return lax.dot_general(
        a, b, (((1,), (0,)), ((), ())), precision=precision, preferred_element_type=F32
    )


def mm_nt(a, b, precision=HIGHEST):
    return lax.dot_general(
        a, b, (((1,), (1,)), ((), ())), precision=precision, preferred_element_type=F32
    )


def factor(gram_twice):
    size = gram_twice.shape[0]
    rows = lax.broadcasted_iota(jnp.int32, (size, 2 * size), 0)
    lanes = lax.broadcasted_iota(jnp.int32, (size, 2 * size), 1)
    work = jnp.where(lanes < size, gram_twice, jnp.where(lanes - size == rows, 1.0, 0.0))

    def all_sum(mask, value):
        part_sum = jnp.sum(jnp.where(mask, value, 0.0), axis=0, keepdims=True)
        return jnp.sum(part_sum, axis=1, keepdims=True)

    def step(i, carry):
        work, pivots = carry
        k = 2 * i
        n = k + 1
        lane_k, lane_n = lanes == k, lanes == n
        row_is_k, row_is_n = rows == k, rows == n
        column_k = jnp.sum(jnp.where(lane_k, work, 0.0), axis=1, keepdims=True)
        column_n = jnp.sum(jnp.where(lane_n, work, 0.0), axis=1, keepdims=True)
        row_k = jnp.sum(jnp.where(row_is_k, work, 0.0), axis=0, keepdims=True)
        row_n = jnp.sum(jnp.where(row_is_n, work, 0.0), axis=0, keepdims=True)
        pivot_k = all_sum(row_is_k & lane_k, work)
        upper = all_sum(row_is_k & lane_n, work)
        lower = all_sum(row_is_n & lane_k, work)
        corner = all_sum(row_is_n & lane_n, work)
        ratio = lower / pivot_k
        pivot_n = corner - ratio * upper
        row_n = row_n - ratio * row_k
        scale_k = column_k / pivot_k
        scale_n = (column_n - scale_k * upper) / pivot_n
        work = work - jnp.where(rows > k, scale_k * row_k, 0.0)
        work = work - jnp.where(rows > n, scale_n * row_n, 0.0)
        pivots = jnp.where(row_is_k, pivot_k, jnp.where(row_is_n, pivot_n, pivots))
        return (work, pivots)

    work, pivots = lax.fori_loop(0, size // 2, step, (work, jnp.ones_like(work)))
    work = work / jnp.sqrt(pivots)
    upper = jnp.where(rows <= lanes, work, 0.0)[:, :size]
    return (upper, work[:, size:])


def krylov_kernel(
    dims,
    panel_ref,
    start_ref,
    basis_ref,
    new_ref,
    coef_ref,
    tri_ref,
    held,
    start_all,
    part,
    gathered,
    image,
    sib_buf,
    col_buf,
    basis,
    proj_part,
    proj_in,
    proj_col,
    proj_all,
    gram_in,
    gram_col,
    out_part,
    out_buf,
    second_all,
    *rest,
):
    n_row, n_col, total_rows = dims
    stages = n_row.bit_length() - 1
    recvs = rest[:stages]
    (panel_sem, mix_send, mix_recv, misc_sem, sib_sem, col_send, col_recv,
     p_send, p_recv, z_send, z_recv, a_send, a_recv, g_send, g_recv, h_send, h_recv,
     o_send, o_recv, half_send, half_recv, s_send, s_recv) = rest[stages:]
    chunks, rows_here, width = held.shape
    cols = start_all.shape[0] * start_all.shape[1]
    pieces = image.shape[0]
    piece = image.shape[2]
    n_plane = n_row * 2
    row = lax.axis_index("row")
    col = lax.axis_index("col")
    core = lax.axis_index("depth")
    inv_total = 1.0 / total_rows

    def bit_of(value, bit):
        return (value // (1 << bit)) % 2

    def pick(first, second):
        return first * (1 - core) + second * core

    partners = []
    order = 0
    for s in range(stages):
        flips = [row + (1 - 2 * bit_of(row, b)) * (1 << b) for b in (s, stages - 1 - s)]
        partners.append(pick(flips[0], flips[1]))
        bits = pick(bit_of(row, s), bit_of(row, stages - 1 - s))
        order = order * 2 + bits
    plane_me = row * 2 + core
    col_group_me = core * n_col + col

    def plane_device(j):
        target = (plane_me + j) % n_plane
        return target, {"row": target // 2, "depth": target % 2}

    def col_device(j):
        target = (col + j) % n_col
        return target, {"col": target}

    def panel_copy(t):
        first = pl.multiple_of((core * chunks + t) * width, width)
        return pltpu.make_async_copy(
            panel_ref.at[:, pl.ds(first, width)], held.at[t], panel_sem.at[t]
        )

    for t in range(min(LOOK, chunks)):
        panel_copy(t).start()

    basis_first = pl.multiple_of(col_group_me * piece, 8)
    basis_copy = pltpu.make_async_copy(
        basis_ref.at[pl.ds(basis_first, piece), :], basis, misc_sem.at[0]
    )
    own_start = pltpu.make_async_copy(start_ref, start_all.at[core], misc_sem.at[1])
    own_start.start()

    barrier = pltpu.get_barrier_semaphore()
    greeted = 0
    for j in range(1, n_plane):
        pl.semaphore_signal(barrier, inc=1, device_id=plane_device(j)[1], device_id_type=MESH)
        greeted += 1
    for j in range(1, n_col):
        pl.semaphore_signal(barrier, inc=1, device_id=col_device(j)[1], device_id_type=MESH)
        greeted += 1
    pl.semaphore_wait(barrier, greeted)

    def remote(src, dst, send_sem, recv_sem, device):
        return pltpu.make_async_remote_copy(
            src_ref=src,
            dst_ref=dst,
            send_sem=send_sem,
            recv_sem=recv_sem,
            device_id=device,
            device_id_type=MESH,
        )

    sibling = {"depth": 1 - core}
    start_copy = remote(start_ref, start_all.at[core], sib_sem.at[0], sib_sem.at[1], sibling)
    start_copy.start()
    image[...] = jnp.zeros_like(image)
    own_start.wait()
    start_copy.wait()

    def span(s):
        length = n_row >> s
        return (order // length) * length, length

    def reduce_copy(s, t):
        first, length = span(s)
        half = length // 2
        mine = span(s + 1)[0]
        other = first + (first + half - mine)
        return remote(
            part.at[t, pl.ds(other, half)],
            recvs[s].at[t],
            mix_send.at[s, t],
            mix_recv.at[s, t],
            {"row": partners[s]},
        )

    def gather_copy(s, t):
        level = stages - 1 - s
        first, length = span(level + 1)
        region = gathered.at[t, pl.ds(first, length)]
        return remote(
            region, region, mix_send.at[stages + s, t], mix_recv.at[stages + s, t],
            {"row": partners[level]},
        )

    block = rows_here // 4
    per_block = block // piece

    def body(i, carry):
        for s in reversed(range(stages)):
            t = i - LAG * (stages + 1 + s)

            if s < stages - 1:
                @pl.when((t >= 0) & (t < chunks))
                def _():
                    gather_copy(s, t).wait_recv()
                    gather_copy(s + 1, t).start()

        for s in reversed(range(stages)):
            t = i - LAG * (s + 1)

            @pl.when((t >= 0) & (t < chunks))
            def _():
                reduce_copy(s, t).wait_recv()
                first, length = span(s + 1)
                summed = part[t, pl.ds(first, length)] + recvs[s][t]
                if s < stages - 1:
                    part[t, pl.ds(first, length)] = summed
                    reduce_copy(s + 1, t).start()
                else:
                    gathered[t, pl.ds(first, length)] = summed.astype(jnp.bfloat16)
                    gather_copy(0, t).start()

        @pl.when(i < chunks)
        def _():
            @pl.when(i + LOOK < chunks)
            def _():
                panel_copy(i + LOOK).start()

            panel_copy(i).wait()
            lhs = start_all[...].reshape(cols, rows_here)
            mixed = mm(lhs, held[i], None)
            for p in range(n_row):
                part[i, p] = mixed[:, p * LANES : (p + 1) * LANES]
            reduce_copy(0, i).start()

        t = i - LAG * 2 * stages

        @pl.when(t >= 0)
        def _():
            gather_copy(stages - 1, t).wait_recv()
            lhs = jnp.concatenate([gathered[t, p] for p in range(n_row)], axis=1)
            for h in range(4):
                got = mm_nt(lhs, held[t, h * block : (h + 1) * block, :], None)
                for q in range(per_block):
                    image[h * per_block + q] += got[:, q * piece : (q + 1) * piece]

        return carry

    lax.fori_loop(0, chunks + LAG * 2 * stages, body, 0)
    basis_copy.start()

    def half_copy(c):
        return remote(
            image.at[(1 - core) * n_col + c], sib_buf.at[c], half_send.at[c], half_recv.at[c], sibling
        )

    for j in range(1, n_col + 1):
        half_copy((col + j) % n_col).start()
    copies = []
    for j in range(1, n_col):
        target, device = col_device(j)
        half_copy(target).wait_recv()
        sib_buf[target] = sib_buf[target] + image[core * n_col + target]
        copies.append(
            remote(sib_buf.at[target], col_buf.at[col], col_send.at[j], col_recv.at[j], device)
        )
        copies[-1].start()
    half_copy(col).wait_recv()
    col_buf[col] = sib_buf[col] + image[core * n_col + col]

    def drain(t, carry):
        for s in range(stages):
            reduce_copy(s, t).wait_send()
            gather_copy(s, t).wait_send()
        return carry

    lax.fori_loop(0, chunks, drain, 0)
    for c in range(n_col):
        half_copy(c).wait_send()
    basis_copy.wait()
    for copy in copies:
        copy.wait()

    image_t = col_buf[0]
    for c in range(1, n_col):
        image_t = image_t + col_buf[c]

    k_total = basis.shape[1]
    piece_rows, piece_lanes = proj_part.shape[1:]
    lane_blocks = k_total // piece_lanes

    def start_plane(slot, src_of, dst, send, recv):
        made = []
        for j in range(1, n_plane):
            target, device = plane_device(j)
            made.append(remote(src_of(target), dst, send.at[slot, j], recv.at[slot, j], device))
            made[-1].start()
        return made

    def start_cols(slot, src, dst, send, recv):
        made = []
        for j in range(1, n_col):
            target, device = col_device(j)
            made.append(remote(src, dst, send.at[slot, j], recv.at[slot, j], device))
            made[-1].start()
        return made

    def finish(made):
        for copy in made:
            copy.wait()

    def ordered_sum(ref, slot, count):
        total = ref[slot, 0]
        for c in range(1, count):
            total = total + ref[slot, c]
        return total

    def project_start(slot, value):
        for p in range(n_plane):
            lane = (p % lane_blocks) * piece_lanes
            top = (p // lane_blocks) * piece_rows
            proj_part[p] = value[top : top + piece_rows, lane : lane + piece_lanes]
        copies = start_plane(
            slot, lambda target: proj_part.at[target], proj_in.at[slot, plane_me], p_send, p_recv
        )
        proj_in[slot, plane_me] = proj_part[plane_me]
        return copies

    def project_mid(slot, copies):
        finish(copies)
        proj_col[slot, col] = ordered_sum(proj_in, slot, n_plane)
        mine = proj_col.at[slot, col]
        return start_cols(slot, mine, mine, z_send, z_recv)

    def project_end(slot, copies):
        finish(copies)
        proj_all[slot, plane_me] = ordered_sum(proj_col, slot, n_col) * inv_total
        mine = proj_all.at[slot, plane_me]
        return start_plane(slot, lambda target: mine, mine, a_send, a_recv)

    def project_value(slot):
        bands = []
        for top in range(n_plane // lane_blocks):
            bands.append(
                jnp.concatenate(
                    [proj_all[slot, top * lane_blocks + p] for p in range(lane_blocks)], axis=1
                )
            )
        return jnp.concatenate(bands, axis=0) if len(bands) > 1 else bands[0]

    def gram_start(slot, value):
        gram_col[slot, col] = mm_nt(value, jnp.concatenate([value, value], axis=0))
        mine = gram_col.at[slot, col]
        return start_cols(slot, mine, mine, h_send, h_recv)

    def gram_mid(slot, copies):
        finish(copies)
        gram_in[slot, plane_me] = ordered_sum(gram_col, slot, n_col)
        mine = gram_in.at[slot, plane_me]
        return start_plane(slot, lambda target: mine, mine, g_send, g_recv)

    def gram_end(slot, copies):
        finish(copies)
        return ordered_sum(gram_in, slot, n_plane) * inv_total

    copies = project_start(0, mm(image_t, basis[...]))
    copies = project_mid(0, copies)
    finish(project_end(0, copies))
    proj_first = project_value(0)
    remainder = image_t - mm_nt(proj_first, basis[...])

    gram_copies = gram_start(0, remainder)
    copies = project_start(1, mm(remainder, basis[...]))
    gram_copies = gram_mid(0, gram_copies)
    copies = project_mid(1, copies)
    gram_first = gram_end(0, gram_copies)
    copies = project_end(1, copies)
    upper_first, inverse_first = factor(gram_first)
    finish(copies)
    proj_second = project_value(1)
    coef = proj_first + proj_second
    half = coef_ref.shape[0]
    proj_second_rem = remainder - mm_nt(proj_second, basis[...])
    second = mm(inverse_first, proj_second_rem)

    gram_copies = gram_start(1, second)
    second_all[col] = second
    second_copies = []
    for j in range(1, n_col):
        target, device = col_device(j)
        mine = second_all.at[col]
        second_copies.append(remote(mine, mine, s_send.at[j], s_recv.at[j], device))
        second_copies[-1].start()

    @pl.when(core == 0)
    def _():
        coef_ref[...] = coef[:half]

    @pl.when(core == 1)
    def _():
        coef_ref[...] = coef[half:]

    gram_copies = gram_mid(1, gram_copies)
    gram_second = gram_end(1, gram_copies)
    upper_second, inverse_second = factor(gram_second)
    finish(second_copies)
    copies = []
    for c in range(n_col):
        new_t = mm(inverse_second, second_all[c])
        out_part[c, 0] = new_t[:half]
        out_part[c, 1] = new_t[half:]
        copies.append(
            remote(
                out_part.at[c, 1 - core], out_buf.at[core * n_col + c],
                o_send.at[c], o_recv.at[c], sibling,
            )
        )
        copies[-1].start()
    for c in range(n_col):
        out_buf[core * n_col + c] = out_part[c, core]
    tri_ref[...] = mm(upper_second, upper_first)
    finish(copies)
    for q in range(pieces):
        new_ref[:, q * piece : (q + 1) * piece] = out_buf[q]


def per_device(matrix_panel, start_block, stored_basis):
    n_row = lax.axis_size("row")
    n_col = lax.axis_size("col")
    n_core = lax.axis_size("depth")
    rows_here, cols_here = matrix_panel.shape
    half = start_block.shape[1]
    cols = half * n_core
    k_total = stored_basis.shape[1]
    stages = n_row.bit_length() - 1
    width = LANES * n_row
    chunks = cols_here // n_core // width
    pieces = n_col * n_core
    piece = rows_here // pieces
    n_plane = n_row * n_core
    piece_lanes = max(LANES, k_total // n_plane)
    piece_rows = cols * k_total // (n_plane * piece_lanes)
    dma = pltpu.SemaphoreType.DMA
    scratch = [
        pltpu.VMEM((chunks, rows_here, width), jnp.bfloat16),
        pltpu.VMEM((n_core, half, rows_here), jnp.bfloat16),
        pltpu.VMEM((chunks, n_row, cols, LANES), F32),
        pltpu.VMEM((chunks, n_row, cols, LANES), jnp.bfloat16),
        pltpu.VMEM((pieces, cols, piece), F32),
        pltpu.VMEM((n_col, cols, piece), F32),
        pltpu.VMEM((n_col, cols, piece), F32),
        pltpu.VMEM((piece, k_total), F32),
        pltpu.VMEM((n_plane, piece_rows, piece_lanes), F32),
        pltpu.VMEM((2, n_plane, piece_rows, piece_lanes), F32),
        pltpu.VMEM((2, n_col, piece_rows, piece_lanes), F32),
        pltpu.VMEM((2, n_plane, piece_rows, piece_lanes), F32),
        pltpu.VMEM((2, n_plane, cols, 2 * cols), F32),
        pltpu.VMEM((2, n_col, cols, 2 * cols), F32),
        pltpu.VMEM((n_col, n_core, half, piece), F32),
        pltpu.VMEM((pieces, half, piece), F32),
        pltpu.VMEM((n_col, cols, piece), F32),
    ]
    scratch += [
        pltpu.VMEM((chunks, n_row >> (s + 1), cols, LANES), F32) for s in range(stages)
    ]
    scratch += [
        dma((chunks,)),
        dma((2 * stages, chunks)),
        dma((2 * stages, chunks)),
        dma((2,)),
        dma((2,)),
        dma((n_col,)),
        dma((n_col,)),
        dma((2, n_plane)),
        dma((2, n_plane)),
        dma((2, n_col)),
        dma((2, n_col)),
        dma((2, n_plane)),
        dma((2, n_plane)),
        dma((2, n_plane)),
        dma((2, n_plane)),
        dma((2, n_col)),
        dma((2, n_col)),
        dma((n_col,)),
        dma((n_col,)),
        dma((n_col,)),
        dma((n_col,)),
        dma((n_col,)),
        dma((n_col,)),
    ]
    whole = pl.BlockSpec(memory_space=pltpu.VMEM)
    hbm = pl.BlockSpec(memory_space=pl.ANY)
    new_t, coef_t, triangle = pl.pallas_call(
        functools.partial(krylov_kernel, (n_row, n_col, rows_here * n_row)),
        out_shape=(
            jax.ShapeDtypeStruct((half, rows_here), F32),
            jax.ShapeDtypeStruct((half, k_total), F32),
            jax.ShapeDtypeStruct((cols, cols), F32),
        ),
        in_specs=[hbm, whole, hbm],
        out_specs=(whole, whole, whole),
        scratch_shapes=scratch,
        compiler_params=pltpu.CompilerParams(
            collective_id=0, has_side_effects=True, vmem_limit_bytes=63 << 20
        ),
    )(matrix_panel, start_block.T, stored_basis)
    return (new_t.T, coef_t.T, triangle)


def solution(mesh):
    placed = (P("row", "col"), P("row", "depth"), P("row", None))
    return jax.shard_map(
        per_device,
        mesh=mesh,
        in_specs=placed,
        out_specs=(P("row", "depth"), P(None, "depth"), P()),
        check_vma=False,
    )
```
